32 devices in a mesh: clip: 2 (over y), seq: 4 (over z), tm: 2 (over x), chan: 2 (over core).
Axes of the slice: x: 2, y: 2, z: 4, core: 2. Of those that a mesh axis runs over, the one named last changes fastest.
Arguments:
- latents: bfloat16 [4, 16, 28800], P(('clip', 'tm'), None, 'seq'), parts along dimension 0, may hold values from -6 to 6
- conv_in: bfloat16 [3, 3, 3, 16, 512], P(None, None, None, None, 'chan'), may hold values from -0.3125 to 0.3125
- conv_up: bfloat16 [3, 3, 3, 512, 256], P(None, None, None, None, 'chan'), may hold values from -0.0546875 to 0.0546875
- to_pixels: bfloat16 [256, 12], P('chan'), may hold values from -0.375 to 0.375
- slot_anchor: int32 [4, 3, 16], P(('clip', 'tm'), None, 'seq'), parts along dimension 0, may hold values from 0 to 144, as said below
- slot_count: int32 [4, 4], P(('clip', 'tm'), 'seq'), parts along dimension 0, may hold values from 1 to 4, 8 in all within a row
Outputs:
- pixels: bfloat16 [4, 16, 3, 1, 128], P(('clip', 'tm'), 'seq'), parts along dimension 0
The draws below stay inside these ranges and needn't reach their ends.
There are 2 independent parts, one for each index of `clip`. The reference program is written for one: setup_inputs(seed, part) draws one part's arguments, and reference() takes and returns one part's arrays. A program takes and returns all parts, laid end to end along the dimension named above; an argument that names none is the same for every part. Nothing has to cross between parts.
Inputs may be any that keep to these rules, and one draw needn't show every extreme that they name: `slot_count`: over the devices of one temporal group the counts sum to 2 times the number of devices; the largest count of each group is 4. `slot_anchor`: component 0 is a frame from 0 to 3, component 1 a row from 0 to 43, component 2 a column from 0 to 144; tiles may intersect; slots at or past a device's count are unused.
All inputs are finite; a program needn't handle non-finite values.
Results may differ from the reference program's by a relative error of at most 0.0059.
Values may be sent and summed in bfloat16 or wider, within the bound.
A program may use at most 64 MiB of HBM per device.

```python
import math
import jax
import jax.numpy as jnp
import numpy as np
from jax import lax

C_LAT = 16
C_MID = 512
C_UP = 256
PIX = 12
H_LAT = 45
W_LAT = 160
FG = 4
TF = 1
TH = 2
TW = 16
TPD = 2
MAXT = 4
GROUPS = 2
SLOTS = 16
GROUP_TOK = 28800
N_SEQ = 4


def draw_slot_anchor(key, part):
    keys = jax.random.split(key, 3)
    frames = jax.random.randint(keys[0], (GROUPS, 1, SLOTS), 0, FG - TF + 1)
    row_part = jax.random.randint(keys[1], (GROUPS, 1, SLOTS), 0, H_LAT - TH + 1)
    col_part = jax.random.randint(keys[2], (GROUPS, 1, SLOTS), 0, W_LAT - TW + 1)
    result = jnp.concatenate([frames, row_part, col_part], axis=1).astype(jnp.int32)
    result = result.at[0, 2, 0].set(W_LAT - TW)
    return result.at[0, 0, 1].set(0)


def levels(key, shape, pieces, least, high):
    loudness, own = 1.0, jax.random.fold_in(key, 6)
    for axis_at, parts in pieces:
        draws = jnp.exp(jax.random.uniform(jax.random.fold_in(own, axis_at), (parts,), jnp.float32, least / len(pieces), high / len(pieces)))
        loudness = loudness * jnp.repeat(draws, shape[axis_at] // parts).reshape([-1 if axis == axis_at else 1 for axis in range(len(shape))])
    return loudness


def split_up(amount, total, most, lean):
    loads = [(1 << 20) // math.isqrt(grade ** lean) + 1 for grade in range(2, amount + 1)]
    spare, holding = total - most - (amount - 1), [1] * (amount - 1)
    while spare > 0:
        movable = [i for i in range(amount - 1) if holding[i] < most]
        pool, left = sum([loads[i] for i in movable]), spare
        for i in movable:
            more = min(most - holding[i], max(1, left * loads[i] // pool), spare)
            holding[i] = holding[i] + more
            spare = spare - more
    return np.array([most] + holding)


def uneven(own_key, amount, total, reach, lean):
    if amount == 2:
        one = jax.random.randint(own_key, (), max(1, total - reach), min(reach, total - 1) + 1)
        return jnp.stack([one, total - one])
    tallies = jnp.asarray(split_up(amount, total, reach, lean), jnp.int32)
    pairs = (amount - 1) // 2
    source_of, receiver = tallies[1:1 + 2 * pairs:2], tallies[2:2 + 2 * pairs:2]
    slack = jnp.minimum(source_of - 1, reach - receiver)
    shifted = jax.random.randint(jax.random.fold_in(own_key, 1), (pairs,), 0, 1 << 20) % (slack + 1)
    tallies = tallies.at[1:1 + 2 * pairs:2].set(source_of - shifted).at[2:2 + 2 * pairs:2].set(receiver + shifted)
    return tallies[jax.random.permutation(jax.random.fold_in(own_key, 2), amount)]


def bell_draw(stream_key, shape, width, bound, shards=(), held_as=jnp.bfloat16):
    drawn = jax.random.normal(stream_key, shape, jnp.float32) * width
    if len(shards) > 0:
        drawn = levels(stream_key, shape, shards, -0.22, 0.18) * drawn
    return jnp.clip(drawn, min=-bound, max=bound).astype(held_as)


def setup_inputs(seed: int = 0, part: int = 0) -> dict:
    key_list = jax.random.split(jax.random.key(seed), 7)
    own_keys = jax.random.split(jax.random.fold_in(key_list[6], part), 7)
    latents = bell_draw(own_keys[0], (GROUPS, C_LAT, GROUP_TOK), 1.0, 6.0, ((0, 2), (2, 4)))
    conv_in = bell_draw(key_list[1], (3, 3, 3, C_LAT, C_MID), (27 * C_LAT) ** -0.5, 0.3125, ((4, 2),))
    conv_up = bell_draw(key_list[2], (3, 3, 3, C_MID, C_UP), (27 * C_MID) ** -0.5, 0.0546875, ((4, 2),))
    to_pixels = bell_draw(key_list[3], (C_UP, PIX), C_UP ** -0.5, 0.375, ((0, 2),))
    slot_anchor = draw_slot_anchor(jax.random.fold_in(jax.random.fold_in(key_list[6], part), 71), part)
    slot_count = jax.vmap(lambda own: uneven(own, N_SEQ, TPD * N_SEQ, MAXT, 2))(jax.random.split(own_keys[5], GROUPS)).reshape((GROUPS, N_SEQ)).astype(jnp.int32)
    return dict(latents=latents, conv_in=conv_in, conv_up=conv_up, to_pixels=to_pixels, slot_anchor=slot_anchor, slot_count=slot_count)


def edge_mask(row_start, col_start, span_h, span_w):
    row_ids = row_start + jnp.arange(span_h, dtype=jnp.int32)
    col_ids = col_start + jnp.arange(span_w, dtype=jnp.int32)
    row_in = (row_ids >= 0) & (row_ids < H_LAT)
    col_in = (col_ids >= 0) & (col_ids < W_LAT)
    return (row_in[:, None] & col_in[None, :]).astype(jnp.float32)


def convolve(volume, kernel, layout):
    return lax.conv_general_dilated(volume, kernel, (1, 1, 1), "VALID", dimension_numbers=(layout, "DHWIO", "NDHWC"), precision=lax.Precision.HIGHEST)


def decode_tile(window, row_start, col_start, kernel_in, kernel_up, to_pixels):
    pre_act = convolve(window[None], kernel_in, "NCDHW")[0]
    edge_keep = edge_mask(row_start - 1, col_start - 1, TH + 2, TW + 2)
    hidden = (jax.nn.silu(pre_act) * edge_keep[None, :, :, None]).astype(jnp.bfloat16)
    hidden = lax.optimization_barrier(hidden).astype(jnp.float32)
    mid_pre = convolve(hidden[None], kernel_up, "NDHWC")[0]
    upper = jax.nn.silu(mid_pre).astype(jnp.bfloat16)
    colors = jnp.dot(upper.reshape(-1, C_UP), to_pixels, preferred_element_type=jnp.float32)
    shaped = colors.reshape(TF, TH, TW, 3, 2, 2).transpose(3, 0, 1, 4, 2, 5).reshape(3, TF, 4 * TH * TW)
    return shaped.astype(jnp.bfloat16)


def reference(latents, conv_in, conv_up, to_pixels, slot_anchor, slot_count):
    kernel_in = conv_in.astype(jnp.float32)
    kernel_up = conv_up.astype(jnp.float32)
    video = latents.reshape(GROUPS, C_LAT, FG, H_LAT, W_LAT).transpose(1, 0, 2, 3, 4)
    video = video.reshape(C_LAT, GROUPS * FG, H_LAT, W_LAT)
    padded = jnp.pad(video, ((0, 0), (4, 0), (2, 2), (2, 2)))
    offsets = jnp.cumsum(slot_count, axis=1) - slot_count
    item_ids = jnp.arange(TPD * N_SEQ, dtype=jnp.int32)
    owners = jnp.sum((offsets[:, None, :] <= item_ids[None, :, None]).astype(jnp.int32), axis=2) - 1
    columns = (owners * MAXT + item_ids[None, :] - jnp.take_along_axis(offsets, owners, axis=1)).astype(jnp.int32)
    group_ids = jnp.broadcast_to(jnp.arange(GROUPS, dtype=jnp.int32)[:, None], columns.shape)
    anchors = jnp.take_along_axis(slot_anchor, jnp.repeat(columns[:, None, :], 3, axis=1), axis=2)
    flat_groups = group_ids.reshape(-1)
    flat_anchors = anchors.transpose(0, 2, 1).reshape(-1, 3).astype(jnp.int32)
    zero_index = jnp.zeros((), jnp.int32)

    def one_item(packed):
        group, anchor = packed
        start = (group * FG + anchor[0]).astype(jnp.int32)
        window = lax.dynamic_slice(padded, (zero_index, start, anchor[1], anchor[2]), (C_LAT, TF + 4, TH + 4, TW + 4))
        return decode_tile(window.astype(jnp.float32), anchor[1], anchor[2], kernel_in, kernel_up, to_pixels)

    decoded = lax.map(one_item, (flat_groups, flat_anchors))
    result = jnp.zeros((GROUPS, SLOTS, 3, TF, 4 * TH * TW), jnp.bfloat16)
    return result.at[flat_groups, columns.reshape(-1)].set(decoded)
```

```python
import functools

import jax
import jax.numpy as jnp
from jax import lax
from jax.experimental import pallas as pl
from jax.experimental.pallas import tpu as pltpu
from jax.sharding import PartitionSpec as P

C_LAT = 16
C_MID = 512
H_LAT = 45
W_LAT = 160
FG = 4
TF = 1
TH = 2
TW = 16
MAXT = 4
WIN_H = TH + 4
WIN_W = TW + 4
WIN_F = TF + 4
HID_F = TF + 2
HID_H = TH + 2
HID_ROWS = HID_H * WIN_W
TAPS = 27
LANES = 128
MARGIN = 3
MESH = pl.DeviceIdType.MESH


def pick_windows(tokens, anchors, owner, part_start, limit):
    lane = lax.broadcasted_iota(jnp.int32, (C_LAT, LANES), 1)
    picked = []
    for j in range(MAXT):
        y0 = anchors[owner, 1, 0, j]
        x0 = anchors[owner, 2, 0, j]
        first = (y0 - 2) * W_LAT + x0 - 2 - part_start + MARGIN * LANES
        total = jnp.zeros((C_LAT, LANES), jnp.float32)
        for r in range(WIN_H):
            at = jnp.clip(first + r * W_LAT, 0, limit)
            block = lax.shift_right_logical(at, 7)
            inside = at & (LANES - 1)
            joined = jnp.where(lane >= inside, tokens[block], tokens[block + 1])
            turned = pltpu.roll(joined, (r * WIN_W - inside) & (LANES - 1), 1)
            total = jnp.where((lane >= r * WIN_W) & (lane < (r + 1) * WIN_W), turned, total)
        picked.append(total.astype(jnp.bfloat16))
    return jnp.concatenate(picked, axis=0)


def grid_of(ids):
    row = jnp.zeros(ids.shape, jnp.int32)
    for r in range(1, WIN_H + 1):
        row = row + (ids >= r * WIN_W).astype(jnp.int32)
    return row, ids - row * WIN_W


def gate(half):
    return half + half * jnp.tanh(half)


def kernel(
    sizes, lat_ref, in_ref, up_ref, pix_ref, anchor_ref, count_ref, out_ref,
    lat, pix, tokens, anchors_cur, anchors_next, send_cur, send_next, received, w_in, w_up, patches, rows_in, hidden, sums, spread,
    part_mine, part_other,
    anchor_send, anchor_recv, next_send, next_recv, win_send, win_recv, wnext_send, wnext_recv,
    load_sems, up_sems, pair_sems,
):
    seq_size, tm_size, shard_len = sizes
    per_frame = seq_size // FG
    seq = lax.axis_index("seq")
    tm = lax.axis_index("tm")
    chan = lax.axis_index("chan")
    has_next = tm < tm_size - 1
    has_prev = tm > 0
    other = {"chan": 1 - chan}

    barrier = pltpu.get_barrier_semaphore()
    pl.semaphore_signal(barrier, inc=1, device_id=other, device_id_type=MESH)
    for step in range(1, seq_size):
        pl.semaphore_signal(
            barrier, inc=1, device_id={"seq": (seq + step) % seq_size}, device_id_type=MESH)

    @pl.when(has_next)
    def _():
        for step in range(seq_size):
            pl.semaphore_signal(
                barrier, inc=1, device_id={"seq": (seq + step) % seq_size, "tm": tm + 1}, device_id_type=MESH)

    @pl.when(has_prev)
    def _():
        for step in range(seq_size):
            pl.semaphore_signal(
                barrier, inc=1, device_id={"seq": (seq + step) % seq_size, "tm": tm - 1}, device_id_type=MESH)

    load_up = [pltpu.make_async_copy(up_ref.at[:, c], w_up.at[c], up_sems.at[c]) for c in range(3)]
    load_in = pltpu.make_async_copy(in_ref, w_in.at[chan], load_sems.at[1])
    load_anchor = pltpu.make_async_copy(anchor_ref, anchors_cur.at[seq], load_sems.at[2])
    load_lat = pltpu.make_async_copy(lat_ref, lat, load_sems.at[4])
    load_pix = pltpu.make_async_copy(pix_ref, pix, load_sems.at[5])
    load_anchor.start()
    load_lat.start()
    load_pix.start()
    load_in.start()
    for copy in load_up:
        copy.start()

    @pl.when(tm == 0)
    def _():
        received[pl.ds(0, seq_size)] = jnp.zeros((seq_size, MAXT * C_LAT, LANES), jnp.bfloat16)

    @pl.when(has_next & has_prev)
    def _():
        pl.semaphore_wait(barrier, 3 * seq_size)

    @pl.when(has_next != has_prev)
    def _():
        pl.semaphore_wait(barrier, 2 * seq_size)

    def anchor_copy(step):
        return pltpu.make_async_remote_copy(
            src_ref=anchor_ref, dst_ref=anchors_cur.at[seq],
            send_sem=anchor_send.at[step], recv_sem=anchor_recv.at[step],
            device_id={"seq": (seq + step) % seq_size}, device_id_type=MESH)

    def anchor_back(step):
        return pltpu.make_async_remote_copy(
            src_ref=anchor_ref, dst_ref=anchors_next.at[seq],
            send_sem=next_send.at[step], recv_sem=next_recv.at[step],
            device_id={"seq": (seq + step) % seq_size, "tm": tm - 1}, device_id_type=MESH)

    def window_copy(step):
        to = (seq + step) % seq_size
        return pltpu.make_async_remote_copy(
            src_ref=send_cur.at[to], dst_ref=received.at[seq_size + seq],
            send_sem=win_send.at[step], recv_sem=win_recv.at[step],
            device_id={"seq": to}, device_id_type=MESH)

    def window_on(step):
        to = (seq + step) % seq_size
        return pltpu.make_async_remote_copy(
            src_ref=send_next.at[to], dst_ref=received.at[seq],
            send_sem=wnext_send.at[step], recv_sem=wnext_recv.at[step],
            device_id={"seq": to, "tm": tm + 1}, device_id_type=MESH)

    @pl.when(has_prev)
    def _():
        for step in range(seq_size):
            anchor_back(step).start()

    for step in range(1, seq_size):
        anchor_copy(step).start()

    pair_in = pltpu.make_async_remote_copy(
        src_ref=in_ref, dst_ref=w_in.at[chan],
        send_sem=pair_sems.at[0], recv_sem=pair_sems.at[1],
        device_id=other, device_id_type=MESH)
    pair_in.start()

    load_lat.wait()
    blocks = tokens.shape[0]
    whole = shard_len // LANES
    rest = shard_len - whole * LANES
    for b in list(range(MARGIN)) + list(range(MARGIN + whole, blocks)):
        tokens[b] = jnp.zeros((C_LAT, LANES), jnp.float32)
    for b in range(whole):
        tokens[MARGIN + b] = lat[:, b * LANES:(b + 1) * LANES].astype(jnp.float32)
    if rest:
        tokens[MARGIN + whole, :, 0:rest] = lat[:, whole * LANES:].astype(jnp.float32)

    part_start = seq % per_frame * shard_len
    limit = (blocks - 2) * LANES + LANES - 1

    load_anchor.wait()
    received[seq_size + seq] = pick_windows(tokens, anchors_cur, seq, part_start, limit)
    for step in range(1, seq_size):
        anchor_copy(step).wait_recv()
    @pl.loop(1, seq_size)
    def _(step):
        to = (seq + step) % seq_size
        send_cur[to] = pick_windows(tokens, anchors_cur, to, part_start, limit)
        window_copy(step).start()

    @pl.when(has_next)
    def _():
        for step in range(seq_size):
            anchor_back(step).wait_recv()

        @pl.loop(0, seq_size)
        def _(step):
            to = (seq + step) % seq_size
            send_next[to] = pick_windows(tokens, anchors_next, to, part_start, limit)
            window_on(step).start()

    load_pix.wait()
    spread[...] = jnp.zeros(spread.shape, jnp.bfloat16)
    row = lax.broadcasted_iota(jnp.int32, (TH * TW, LANES), 0)
    col = lax.broadcasted_iota(jnp.int32, (TH * TW, LANES), 1)
    for i in range(4):
        target = (2 * (row >> 4) + i // 2) * (2 * TW) + 2 * (row & 15) + i % 2
        chosen = (target == col).astype(jnp.float32).astype(jnp.bfloat16)
        for j in range(MAXT):
            spread[i * LANES + j * TH * TW:i * LANES + (j + 1) * TH * TW, j * LANES:(j + 1) * LANES] = chosen
    k_id = lax.broadcasted_iota(jnp.int32, (32, 12), 1)
    o_id = lax.broadcasted_iota(jnp.int32, (32, 12), 0)
    order = ((k_id >> 2) + (k_id & 3) * 8 == o_id).astype(jnp.float32).astype(jnp.bfloat16)
    to_pix = jnp.dot(order, pix[...], preferred_element_type=jnp.float32).astype(jnp.bfloat16)

    for step in range(1, seq_size):
        window_copy(step).wait_recv()

    @pl.when(has_prev)
    def _():
        for step in range(seq_size):
            window_on(step).wait_recv()

    lane = lax.broadcasted_iota(jnp.int32, (C_LAT, LANES), 1)
    win_row, win_col = grid_of(lane)
    for j in range(MAXT):
        f0, y0, x0 = (anchors_cur[seq, i, 0, j] for i in range(3))
        row_at, col_at = win_row + (y0 - 2), win_col + (x0 - 2)
        keep = (row_at >= 0) & (row_at < H_LAT) & (col_at >= 0) & (col_at < W_LAT) & (win_row < WIN_H)
        token = row_at * W_LAT + col_at
        for k in range(WIN_F):
            window = jnp.zeros((C_LAT, LANES), jnp.float32)
            for part in range(per_frame):
                held = received[(f0 + k) * per_frame + part, pl.ds(j * C_LAT, C_LAT), :].astype(jnp.float32)
                mine = keep
                if per_frame > 1:
                    mine = keep & (token >= part * shard_len) & (token < (part + 1) * shard_len)
                window = jnp.where(mine, held, window)
            for b in range(3):
                for c in range(3):
                    shift = b * WIN_W + c
                    moved = window if shift == 0 else pltpu.roll(window, LANES - shift, 1)
                    moved = moved.astype(jnp.bfloat16)
                    for a in range(3):
                        t = k - a
                        if 0 <= t < HID_F:
                            tap = (a * 3 + b) * 3 + c
                            patches[j * HID_F + t, pl.ds(tap * C_LAT, C_LAT), :] = moved

    load_in.wait()
    pair_in.wait_recv()

    hid_ids = lax.broadcasted_iota(jnp.int32, (HID_ROWS, LANES), 0)
    hid_row, hid_col = grid_of(hid_ids)
    halves = []
    for j in range(MAXT):
        y0, x0 = anchors_cur[seq, 1, 0, j], anchors_cur[seq, 2, 0, j]
        row_at, col_at = hid_row + (y0 - 1), hid_col + (x0 - 1)
        keep = (row_at >= 0) & (row_at < H_LAT) & (col_at >= 0) & (col_at < W_LAT)
        halves.append(jnp.where(keep, 0.5, 0.0))
    for i in range(MAXT * HID_F):
        rows_in[i * HID_ROWS:(i + 1) * HID_ROWS, :] = patches[i].T[:HID_ROWS]
    for half in range(2):
        pre = jnp.dot(rows_in[...], w_in[half], preferred_element_type=jnp.float32)
        for i in range(MAXT * HID_F):
            for part in range(2):
                piece = pre[i * HID_ROWS:(i + 1) * HID_ROWS, part * LANES:(part + 1) * LANES]
                hidden[i, half * 2 + part, 0:HID_ROWS, :] = gate(piece * halves[i // HID_F])

    for copy in load_up:
        copy.wait()
    taken = TH * WIN_W
    rows = []
    for j in range(MAXT):
        pieces = [
            hidden[j * HID_F + a, part, b * WIN_W:b * WIN_W + taken, :]
            for a in range(3) for b in range(3) for part in range(C_MID // LANES)
        ]
        rows.append(jnp.concatenate(pieces, axis=1))
    rows = jnp.concatenate(rows, axis=0).astype(jnp.bfloat16)
    weights = jnp.concatenate([w_up[c].reshape(9 * C_MID, LANES) for c in range(3)], axis=1)
    total = jnp.dot(rows, weights, preferred_element_type=jnp.float32)
    for c in range(3):
        sums[c] = total[:, c * LANES:(c + 1) * LANES]
    moved = []
    for j in range(MAXT):
        for y in range(TH):
            at = j * taken + y * WIN_W
            moved.append(sums[0, at:at + TW, :] + sums[1, at + 1:at + 1 + TW, :] + sums[2, at + 2:at + 2 + TW, :])
    upper = gate(jnp.concatenate(moved, axis=0) * 0.5).astype(jnp.bfloat16)
    part_mine[...] = lax.dot_general(
        to_pix, upper, (((1,), (1,)), ((), ())), preferred_element_type=jnp.float32)
    pair_out = pltpu.make_async_remote_copy(
        src_ref=part_mine, dst_ref=part_other,
        send_sem=pair_sems.at[2], recv_sem=pair_sems.at[3],
        device_id=other, device_id_type=MESH)
    pair_out.start()

    pair_in.wait_send()
    for step in range(1, seq_size):
        anchor_copy(step).wait_send()
        window_copy(step).wait_send()

    @pl.when(has_prev)
    def _():
        for step in range(seq_size):
            anchor_back(step).wait_send()

    @pl.when(has_next)
    def _():
        for step in range(seq_size):
            window_on(step).wait_send()

    pair_out.wait()
    colors = part_mine[...] + part_other[...]
    wide = jnp.concatenate([colors[8 * i:8 * (i + 1)] for i in range(4)], axis=1).astype(jnp.bfloat16)
    shuffled = jnp.dot(wide, spread[...], preferred_element_type=jnp.float32)
    live = lax.broadcasted_iota(jnp.int32, (MAXT, LANES), 0) < count_ref[0, 0]
    for e in range(3):
        tiles = [shuffled[e:e + 1, j * LANES:(j + 1) * LANES] for j in range(MAXT)]
        out_ref[e] = jnp.where(live, jnp.concatenate(tiles, axis=0), 0.0).astype(jnp.bfloat16)


def local(latents, conv_in, conv_up, to_pixels, slot_anchor, slot_count):
    seq_size = lax.axis_size("seq")
    tm_size = lax.axis_size("tm")
    shard_len = latents.shape[2]
    blocks = MARGIN + (shard_len + LANES - 1) // LANES + 3
    dma = pltpu.SemaphoreType.DMA
    vmem = pl.BlockSpec(memory_space=pltpu.VMEM)
    hbm = pl.BlockSpec(memory_space=pltpu.HBM)
    result = pl.pallas_call(
        functools.partial(kernel, (seq_size, tm_size, shard_len)),
        out_shape=pltpu.VMEM((3, MAXT, LANES), jnp.bfloat16),
        in_specs=[hbm] * 5 + [pl.BlockSpec(memory_space=pltpu.SMEM)],
        out_specs=vmem,
        scratch_shapes=[
            pltpu.VMEM((C_LAT, shard_len), jnp.bfloat16),
            pltpu.VMEM(to_pixels.shape[::-1], jnp.bfloat16),
            pltpu.VMEM((blocks, C_LAT, LANES), jnp.float32),
            pltpu.SMEM((seq_size, 3, 1, MAXT), jnp.int32),
            pltpu.SMEM((seq_size, 3, 1, MAXT), jnp.int32),
            pltpu.VMEM((seq_size, MAXT * C_LAT, LANES), jnp.bfloat16),
            pltpu.VMEM((seq_size, MAXT * C_LAT, LANES), jnp.bfloat16),
            pltpu.VMEM((2 * seq_size, MAXT * C_LAT, LANES), jnp.bfloat16),
            pltpu.VMEM((2, TAPS * C_LAT, 256), jnp.bfloat16),
            pltpu.VMEM((3, 9, C_MID, LANES), jnp.bfloat16),
            pltpu.VMEM((MAXT * HID_F, TAPS * C_LAT, LANES), jnp.bfloat16),
            pltpu.VMEM((MAXT * HID_F * HID_ROWS, TAPS * C_LAT), jnp.bfloat16),
            pltpu.VMEM((MAXT * HID_F, C_MID // LANES, HID_ROWS, LANES), jnp.float32),
            pltpu.VMEM((3, MAXT * TH * WIN_W, LANES), jnp.float32),
            pltpu.VMEM((4 * LANES, MAXT * LANES), jnp.bfloat16),
            pltpu.VMEM((32, LANES), jnp.float32),
            pltpu.VMEM((32, LANES), jnp.float32),
            dma((seq_size,)), dma((seq_size,)), dma((seq_size,)), dma((seq_size,)),
            dma((seq_size,)), dma((seq_size,)), dma((seq_size,)), dma((seq_size,)),
            dma((6,)), dma((3,)), dma((4,)),
        ],
        compiler_params=pltpu.CompilerParams(collective_id=0, has_side_effects=True),
        name="decode",
    )(
        latents[0], conv_in.reshape(TAPS * C_LAT, -1), conv_up.reshape(9, 3, C_MID, -1),
        to_pixels.T, slot_anchor.transpose(1, 0, 2), slot_count)
    return result.transpose(1, 0, 2)[None, :, :, None, :]


def solution(mesh):
    placed = (
        P(("clip", "tm"), None, "seq"),
        P(None, None, None, None, "chan"),
        P(None, None, None, None, "chan"),
        P("chan", None),
        P(("clip", "tm"), None, "seq"),
        P(("clip", "tm"), "seq"),
    )
    return jax.shard_map(
        local,
        mesh=mesh,
        in_specs=placed,
        out_specs=P(("clip", "tm"), "seq", None, None, None),
        check_vma=False,
    )
```

```python
import functools

import jax
import jax.numpy as jnp
from jax import lax
from jax.experimental import pallas as pl
from jax.experimental.pallas import tpu as pltpu
from jax.sharding import PartitionSpec as P

C_LAT = 16
C_MID = 512
H_LAT = 45
W_LAT = 160
FG = 4
TF = 1
TH = 2
TW = 16
MAXT = 4
WIN_H = TH + 4
WIN_W = TW + 4
WIN_F = TF + 4
HID_F = TF + 2
HID_H = TH + 2
HID_ROWS = HID_H * WIN_W
TAPS = 27
LANES = 128
MARGIN = 3
HELD = MAXT // 2
MESH = pl.DeviceIdType.MESH


def pick_windows(tokens, anchors, owner, slots, part_start, limit):
    lane = lax.broadcasted_iota(jnp.int32, (C_LAT, LANES), 1)
    picked = []
    for j in range(HELD):
        y0 = anchors[owner, 1, 0, slots + j]
        x0 = anchors[owner, 2, 0, slots + j]
        first = (y0 - 2) * W_LAT + x0 - 2 - part_start + MARGIN * LANES
        total = jnp.zeros((C_LAT, LANES), jnp.float32)
        for r in range(WIN_H):
            at = jnp.clip(first + r * W_LAT, 0, limit)
            block = lax.shift_right_logical(at, 7)
            inside = at & (LANES - 1)
            joined = jnp.where(lane >= inside, tokens[block], tokens[block + 1])
            turned = pltpu.roll(joined, (r * WIN_W - inside) & (LANES - 1), 1)
            total = jnp.where((lane >= r * WIN_W) & (lane < (r + 1) * WIN_W), turned, total)
        picked.append(total.astype(jnp.bfloat16))
    return jnp.concatenate(picked, axis=0)


def grid_of(ids):
    row = jnp.zeros(ids.shape, jnp.int32)
    for r in range(1, WIN_H + 1):
        row = row + (ids >= r * WIN_W).astype(jnp.int32)
    return row, ids - row * WIN_W


def gate(half):
    return half + half * jnp.tanh(half)


def kernel(
    sizes, lat_ref, in_ref, up_ref, pix_ref, anchor_ref, count_ref, out_ref,
    lat, pix, tokens, anchors_cur, anchors_next, send_cur, send_next, received, w_in, w_up, patches, rows_in, hidden,
    spread, parts,
    anchor_send, anchor_recv, next_send, next_recv, win_send, win_recv, wnext_send, wnext_recv,
    load_sems, pair_sems,
):
    seq_size, tm_size, shard_len = sizes
    per_frame = seq_size // FG
    seq = lax.axis_index("seq")
    tm = lax.axis_index("tm")
    chan = lax.axis_index("chan")
    has_next = tm < tm_size - 1
    has_prev = tm > 0
    other = {"chan": 1 - chan}
    slots = chan * HELD

    barrier = pltpu.get_barrier_semaphore()
    pl.semaphore_signal(barrier, inc=1, device_id=other, device_id_type=MESH)
    for step in range(1, seq_size):
        pl.semaphore_signal(
            barrier, inc=1, device_id={"seq": (seq + step) % seq_size}, device_id_type=MESH)

    @pl.when(has_next)
    def _():
        for step in range(seq_size):
            pl.semaphore_signal(
                barrier, inc=1, device_id={"seq": (seq + step) % seq_size, "tm": tm + 1}, device_id_type=MESH)

    load_up = pltpu.make_async_copy(up_ref, w_up.at[chan], load_sems.at[0])
    load_in = pltpu.make_async_copy(in_ref, w_in.at[chan], load_sems.at[1])
    load_anchor = pltpu.make_async_copy(anchor_ref, anchors_cur.at[seq], load_sems.at[2])
    load_lat = pltpu.make_async_copy(lat_ref, lat, load_sems.at[4])
    load_pix = pltpu.make_async_copy(pix_ref, pix.at[chan], load_sems.at[5])
    load_anchor.start()
    load_lat.start()
    load_pix.start()
    load_in.start()
    load_up.start()

    @pl.when(tm == 0)
    def _():
        received[pl.ds(0, seq_size)] = jnp.zeros((seq_size, HELD * C_LAT, LANES), jnp.bfloat16)

    @pl.when(has_prev)
    def _():
        pl.semaphore_wait(barrier, 2 * seq_size)

    @pl.when(tm == 0)
    def _():
        pl.semaphore_wait(barrier, seq_size)

    def anchor_copy(step):
        return pltpu.make_async_remote_copy(
            src_ref=anchor_ref, dst_ref=anchors_cur.at[seq],
            send_sem=anchor_send.at[step], recv_sem=anchor_recv.at[step],
            device_id={"seq": (seq + step) % seq_size}, device_id_type=MESH)

    def anchor_back(step):
        return pltpu.make_async_remote_copy(
            src_ref=anchor_ref, dst_ref=anchors_next.at[seq],
            send_sem=next_send.at[step], recv_sem=next_recv.at[step],
            device_id={"seq": (seq + step) % seq_size, "tm": tm - 1}, device_id_type=MESH)

    def window_copy(step):
        to = (seq + step) % seq_size
        return pltpu.make_async_remote_copy(
            src_ref=send_cur.at[to], dst_ref=received.at[seq_size + seq],
            send_sem=win_send.at[step], recv_sem=win_recv.at[step],
            device_id={"seq": to}, device_id_type=MESH)

    def window_on(step):
        to = (seq + step) % seq_size
        return pltpu.make_async_remote_copy(
            src_ref=send_next.at[to], dst_ref=received.at[seq],
            send_sem=wnext_send.at[step], recv_sem=wnext_recv.at[step],
            device_id={"seq": to, "tm": tm + 1}, device_id_type=MESH)

    for step in range(1, seq_size):
        anchor_copy(step).start()

    @pl.when(has_prev)
    def _():
        for step in range(seq_size):
            anchor_back(step).start()

    def pair_copy(src, dst, at):
        return pltpu.make_async_remote_copy(
            src_ref=src, dst_ref=dst, send_sem=pair_sems.at[2 * at], recv_sem=pair_sems.at[2 * at + 1],
            device_id=other, device_id_type=MESH)

    pair_in = pair_copy(in_ref, w_in.at[chan], 0)
    pair_pix = pair_copy(pix_ref, pix.at[chan], 1)
    pair_up = pair_copy(up_ref, w_up.at[chan], 2)
    pair_in.start()
    pair_pix.start()
    pair_up.start()

    load_lat.wait()
    blocks = tokens.shape[0]
    whole = shard_len // LANES
    rest = shard_len - whole * LANES
    for b in list(range(MARGIN)) + list(range(MARGIN + whole, blocks)):
        tokens[b] = jnp.zeros((C_LAT, LANES), jnp.float32)
    for b in range(whole):
        tokens[MARGIN + b] = lat[:, b * LANES:(b + 1) * LANES].astype(jnp.float32)
    if rest:
        tokens[MARGIN + whole, :, 0:rest] = lat[:, whole * LANES:].astype(jnp.float32)

    part_start = seq % per_frame * shard_len
    limit = (blocks - 2) * LANES + LANES - 1

    load_anchor.wait()
    received[seq_size + seq] = pick_windows(tokens, anchors_cur, seq, slots, part_start, limit)

    upside = 2 * seq // seq_size
    place = seq + upside * (seq_size - 1 - 2 * seq)

    def near_to_far(i):
        at = i + (i + seq_size - place) // seq_size
        return at + upside * (seq_size - 1 - 2 * at)

    def serve_next(to):
        anchor_back((seq - to + seq_size) % seq_size).wait_recv()
        send_next[to] = pick_windows(tokens, anchors_next, to, slots, part_start, limit)
        window_on((to - seq + seq_size) % seq_size).start()

    @pl.loop(0, seq_size - 1)
    def _(i):
        to = near_to_far(i)
        anchor_copy((seq - to + seq_size) % seq_size).wait_recv()
        send_cur[to] = pick_windows(tokens, anchors_cur, to, slots, part_start, limit)
        window_copy((to - seq + seq_size) % seq_size).start()

    @pl.when(has_next)
    def _():
        serve_next(seq)

        @pl.loop(0, seq_size - 1)
        def _(i):
            serve_next(near_to_far(i))

    load_pix.wait()
    pair_pix.wait_recv()
    cells = HELD * TH * TW
    spread[...] = jnp.zeros(spread.shape, jnp.bfloat16)
    row = lax.broadcasted_iota(jnp.int32, (TH * TW, LANES), 0)
    col = lax.broadcasted_iota(jnp.int32, (TH * TW, LANES), 1)
    for i in range(4):
        target = (2 * (row >> 4) + i // 2) * (2 * TW) + 2 * (row & 15) + i % 2
        chosen = (target == col).astype(jnp.float32).astype(jnp.bfloat16)
        for j in range(HELD):
            at = i * cells + j * TH * TW
            spread[at:at + TH * TW, j * LANES:(j + 1) * LANES] = chosen
    k_id = lax.broadcasted_iota(jnp.int32, (32, 12), 1)
    o_id = lax.broadcasted_iota(jnp.int32, (32, 12), 0)
    order = ((k_id >> 2) + (k_id & 3) * 8 == o_id).astype(jnp.float32).astype(jnp.bfloat16)
    to_pix = jnp.dot(
        order, jnp.concatenate([pix[0], pix[1]], axis=1), preferred_element_type=jnp.float32).astype(jnp.bfloat16)

    load_in.wait()
    pair_in.wait_recv()
    load_up.wait()
    pair_up.wait_recv()
    for step in range(1, seq_size):
        window_copy(step).wait_recv()

    @pl.when(has_prev)
    def _():
        for step in range(seq_size):
            window_on(step).wait_recv()

    lane = lax.broadcasted_iota(jnp.int32, (C_LAT, LANES), 1)
    win_row, win_col = grid_of(lane)
    hid_ids = lax.broadcasted_iota(jnp.int32, (HID_ROWS, LANES), 0)
    hid_row, hid_col = grid_of(hid_ids)
    halves = []
    for j in range(HELD):
        f0, y0, x0 = (anchors_cur[seq, i, 0, slots + j] for i in range(3))
        row_at, col_at = hid_row + (y0 - 1), hid_col + (x0 - 1)
        keep = (row_at >= 0) & (row_at < H_LAT) & (col_at >= 0) & (col_at < W_LAT)
        halves.append(jnp.where(keep, 0.5, 0.0))
        row_at, col_at = win_row + (y0 - 2), win_col + (x0 - 2)
        keep = (row_at >= 0) & (row_at < H_LAT) & (col_at >= 0) & (col_at < W_LAT) & (win_row < WIN_H)
        token = row_at * W_LAT + col_at
        for k in range(WIN_F):
            window = jnp.zeros((C_LAT, LANES), jnp.float32)
            for part in range(per_frame):
                held = received[(f0 + k) * per_frame + part, pl.ds(j * C_LAT, C_LAT), :].astype(jnp.float32)
                mine = keep
                if per_frame > 1:
                    mine = keep & (token >= part * shard_len) & (token < (part + 1) * shard_len)
                window = jnp.where(mine, held, window)
            for b in range(3):
                for c in range(3):
                    shift = b * WIN_W + c
                    moved = window if shift == 0 else pltpu.roll(window, LANES - shift, 1)
                    moved = moved.astype(jnp.bfloat16)
                    for a in range(3):
                        t = k - a
                        if 0 <= t < HID_F:
                            tap = (a * 3 + b) * 3 + c
                            patches[j * HID_F + t, pl.ds(tap * C_LAT, C_LAT), :] = moved

    for i in range(HELD * HID_F):
        rows_in[i * HID_ROWS:(i + 1) * HID_ROWS, :] = patches[i].T[:HID_ROWS]
    for half in range(2):
        pre = jnp.dot(rows_in[...], w_in[half], preferred_element_type=jnp.float32)
        for i in range(HELD * HID_F):
            for part in range(2):
                piece = pre[i * HID_ROWS:(i + 1) * HID_ROWS, part * LANES:(part + 1) * LANES]
                hidden[i, half * 2 + part, :, :] = gate(piece * halves[i // HID_F])

    rows = []
    for j in range(HELD):
        for y in range(TH):
            pieces = [
                hidden[j * HID_F + a, part, (y + b) * WIN_W + c:(y + b) * WIN_W + c + TW, :]
                for a in range(3) for b in range(3) for c in range(3) for part in range(C_MID // LANES)
            ]
            rows.append(jnp.concatenate(pieces, axis=1).astype(jnp.bfloat16))
    total = jnp.dot(
        jnp.concatenate(rows, axis=0), jnp.concatenate([w_up[0], w_up[1]], axis=1),
        preferred_element_type=jnp.float32)
    upper = gate(total * 0.5).astype(jnp.bfloat16)
    colors = lax.dot_general(
        to_pix, upper, (((1,), (1,)), ((), ())), preferred_element_type=jnp.float32)
    wide = jnp.concatenate([colors[8 * i:8 * (i + 1)] for i in range(4)], axis=1).astype(jnp.bfloat16)
    parts[chan] = jnp.dot(wide, spread[...], preferred_element_type=jnp.float32)
    pair_out = pair_copy(parts.at[chan], parts.at[chan], 3)
    pair_out.start()

    pair_in.wait_send()
    pair_pix.wait_send()
    pair_up.wait_send()
    for step in range(1, seq_size):
        anchor_copy(step).wait_send()
        window_copy(step).wait_send()

    @pl.when(has_prev)
    def _():
        for step in range(seq_size):
            anchor_back(step).wait_send()

    @pl.when(has_next)
    def _():
        for step in range(seq_size):
            window_on(step).wait_send()

    pair_out.wait()
    live = lax.broadcasted_iota(jnp.int32, (MAXT, LANES), 0) < count_ref[0, 0]
    for e in range(3):
        tiles = [parts[j // HELD, e:e + 1, j % HELD * LANES:(j % HELD + 1) * LANES] for j in range(MAXT)]
        out_ref[e] = jnp.where(live, jnp.concatenate(tiles, axis=0), 0.0).astype(jnp.bfloat16)


def local(latents, conv_in, conv_up, to_pixels, slot_anchor, slot_count):
    seq_size = lax.axis_size("seq")
    tm_size = lax.axis_size("tm")
    shard_len = latents.shape[2]
    blocks = MARGIN + (shard_len + LANES - 1) // LANES + 3
    dma = pltpu.SemaphoreType.DMA
    vmem = pl.BlockSpec(memory_space=pltpu.VMEM)
    hbm = pl.BlockSpec(memory_space=pltpu.HBM)
    result = pl.pallas_call(
        functools.partial(kernel, (seq_size, tm_size, shard_len)),
        out_shape=pltpu.VMEM((3, MAXT, LANES), jnp.bfloat16),
        in_specs=[hbm] * 5 + [pl.BlockSpec(memory_space=pltpu.SMEM)],
        out_specs=vmem,
        scratch_shapes=[
            pltpu.VMEM((C_LAT, shard_len), jnp.bfloat16),
            pltpu.VMEM((2,) + to_pixels.shape[::-1], jnp.bfloat16),
            pltpu.VMEM((blocks, C_LAT, LANES), jnp.float32),
            pltpu.SMEM((seq_size, 3, 1, MAXT), jnp.int32),
            pltpu.SMEM((seq_size, 3, 1, MAXT), jnp.int32),
            pltpu.VMEM((seq_size, HELD * C_LAT, LANES), jnp.bfloat16),
            pltpu.VMEM((seq_size, HELD * C_LAT, LANES), jnp.bfloat16),
            pltpu.VMEM((2 * seq_size, HELD * C_LAT, LANES), jnp.bfloat16),
            pltpu.VMEM((2, TAPS * C_LAT, 256), jnp.bfloat16),
            pltpu.VMEM((2, TAPS * C_MID, LANES), jnp.bfloat16),
            pltpu.VMEM((HELD * HID_F, TAPS * C_LAT, LANES), jnp.bfloat16),
            pltpu.VMEM((HELD * HID_F * HID_ROWS, TAPS * C_LAT), jnp.bfloat16),
            pltpu.VMEM((HELD * HID_F, C_MID // LANES, HID_ROWS, LANES), jnp.float32),
            pltpu.VMEM((4 * HELD * TH * TW, HELD * LANES), jnp.bfloat16),
            pltpu.VMEM((2, 8, HELD * LANES), jnp.float32),
            dma((seq_size,)), dma((seq_size,)), dma((seq_size,)), dma((seq_size,)),
            dma((seq_size,)), dma((seq_size,)), dma((seq_size,)), dma((seq_size,)),
            dma((6,)), dma((8,)),
        ],
        compiler_params=pltpu.CompilerParams(collective_id=0, has_side_effects=True),
        name="decode",
    )(
        latents[0], conv_in.reshape(TAPS * C_LAT, -1), conv_up.reshape(TAPS * C_MID, -1),
        to_pixels.T, slot_anchor.transpose(1, 0, 2), slot_count)
    return result.transpose(1, 0, 2)[None, :, :, None, :]


def solution(mesh):
    placed = (
        P(("clip", "tm"), None, "seq"),
        P(None, None, None, None, "chan"),
        P(None, None, None, None, "chan"),
        P("chan", None),
        P(("clip", "tm"), None, "seq"),
        P(("clip", "tm"), "seq"),
    )
    return jax.shard_map(
        local,
        mesh=mesh,
        in_specs=placed,
        out_specs=P(("clip", "tm"), "seq", None, None, None),
        check_vma=False,
    )
```

```python
import functools

import jax
import jax.numpy as jnp
from jax import lax
from jax.experimental import pallas as pl
from jax.experimental.pallas import tpu as pltpu
from jax.sharding import PartitionSpec as P

C_LAT = 16
C_MID = 512
H_LAT = 45
W_LAT = 160
FG = 4
TF = 1
TH = 2
TW = 16
MAXT = 4
WIN_H = TH + 4
WIN_W = TW + 4
WIN_F = TF + 4
HID_F = TF + 2
HID_H = TH + 2
HID_ROWS = HID_H * WIN_W
TAPS = 27
LANES = 128
MARGIN = 3
HELD = MAXT // 2
MESH = pl.DeviceIdType.MESH


def pick_windows(tokens, anchors, owner, slots, part_start, limit):
    lane = lax.broadcasted_iota(jnp.int32, (C_LAT, LANES), 1)
    picked = []
    for j in range(HELD):
        y0 = anchors[owner, 1, 0, slots + j]
        x0 = anchors[owner, 2, 0, slots + j]
        first = (y0 - 2) * W_LAT + x0 - 2 - part_start + MARGIN * LANES
        total = jnp.zeros((C_LAT, LANES), jnp.float32)
        for r in range(WIN_H):
            at = jnp.clip(first + r * W_LAT, 0, limit)
            block = lax.shift_right_logical(at, 7)
            inside = at & (LANES - 1)
            joined = jnp.where(lane >= inside, tokens[block], tokens[block + 1])
            turned = pltpu.roll(joined, (r * WIN_W - inside) & (LANES - 1), 1)
            total = jnp.where((lane >= r * WIN_W) & (lane < (r + 1) * WIN_W), turned, total)
        picked.append(total.astype(jnp.bfloat16))
    return jnp.concatenate(picked, axis=0)


def grid_of(ids):
    row = jnp.zeros(ids.shape, jnp.int32)
    for r in range(1, WIN_H + 1):
        row = row + (ids >= r * WIN_W).astype(jnp.int32)
    return row, ids - row * WIN_W


def gate(half):
    return half + half * jnp.tanh(half)


def kernel(
    sizes, lat_ref, in_ref, up_ref, pix_ref, anchor_ref, count_ref, out_ref,
    lat, pix, tokens, anchors_cur, anchors_next, send_cur, send_next, received, w_in, w_up, patches, rows_in, hidden,
    spread, parts,
    anchor_send, anchor_recv, next_send, next_recv, win_send, win_recv, wnext_send, wnext_recv,
    load_sems, pair_sems,
):
    seq_size, tm_size, shard_len = sizes
    per_frame = seq_size // FG
    seq = lax.axis_index("seq")
    tm = lax.axis_index("tm")
    chan = lax.axis_index("chan")
    has_next = tm < tm_size - 1
    has_prev = tm > 0
    other = {"chan": 1 - chan}
    slots = chan * HELD

    barrier = pltpu.get_barrier_semaphore()
    pl.semaphore_signal(barrier, inc=1, device_id=other, device_id_type=MESH)
    for step in range(1, seq_size):
        pl.semaphore_signal(
            barrier, inc=1, device_id={"seq": (seq + step) % seq_size}, device_id_type=MESH)

    @pl.when(has_next)
    def _():
        for step in range(seq_size):
            pl.semaphore_signal(
                barrier, inc=1, device_id={"seq": (seq + step) % seq_size, "tm": tm + 1}, device_id_type=MESH)

    load_up = pltpu.make_async_copy(up_ref, w_up.at[chan], load_sems.at[0])
    load_in = pltpu.make_async_copy(in_ref, w_in.at[chan], load_sems.at[1])
    load_anchor = pltpu.make_async_copy(anchor_ref, anchors_cur.at[seq], load_sems.at[2])
    load_lat = pltpu.make_async_copy(lat_ref, lat, load_sems.at[4])
    load_pix = pltpu.make_async_copy(pix_ref, pix.at[chan], load_sems.at[5])
    load_anchor.start()
    load_lat.start()
    load_pix.start()
    load_in.start()
    load_up.start()

    @pl.when(tm == 0)
    def _():
        received[pl.ds(0, seq_size)] = jnp.zeros((seq_size, HELD * C_LAT, LANES), jnp.bfloat16)

    @pl.when(has_prev)
    def _():
        pl.semaphore_wait(barrier, 2 * seq_size)

    @pl.when(tm == 0)
    def _():
        pl.semaphore_wait(barrier, seq_size)

    def anchor_copy(step):
        return pltpu.make_async_remote_copy(
            src_ref=anchor_ref, dst_ref=anchors_cur.at[seq],
            send_sem=anchor_send.at[step], recv_sem=anchor_recv.at[step],
            device_id={"seq": (seq + step) % seq_size}, device_id_type=MESH)

    def anchor_back(step):
        return pltpu.make_async_remote_copy(
            src_ref=anchor_ref, dst_ref=anchors_next.at[seq],
            send_sem=next_send.at[step], recv_sem=next_recv.at[step],
            device_id={"seq": (seq + step) % seq_size, "tm": tm - 1}, device_id_type=MESH)

    def window_copy(step):
        to = (seq + step) % seq_size
        return pltpu.make_async_remote_copy(
            src_ref=send_cur.at[to], dst_ref=received.at[seq_size + seq],
            send_sem=win_send.at[step], recv_sem=win_recv.at[step],
            device_id={"seq": to}, device_id_type=MESH)

    def window_on(step):
        to = (seq + step) % seq_size
        return pltpu.make_async_remote_copy(
            src_ref=send_next.at[to], dst_ref=received.at[seq],
            send_sem=wnext_send.at[step], recv_sem=wnext_recv.at[step],
            device_id={"seq": to, "tm": tm + 1}, device_id_type=MESH)

    upside = 2 * seq // seq_size
    place = seq + upside * (seq_size - 1 - 2 * seq)

    def near_to_far(i):
        at = i + (i + seq_size - place) // seq_size
        return at + upside * (seq_size - 1 - 2 * at)

    @pl.loop(0, seq_size - 1)
    def _(i):
        step = (near_to_far(seq_size - 2 - i) - seq + seq_size) % seq_size

        @pl.when(has_prev)
        def _():
            anchor_back(step).start()

        anchor_copy(step).start()

    @pl.when(has_prev)
    def _():
        anchor_back(0).start()

    def pair_copy(src, dst, at):
        return pltpu.make_async_remote_copy(
            src_ref=src, dst_ref=dst, send_sem=pair_sems.at[2 * at], recv_sem=pair_sems.at[2 * at + 1],
            device_id=other, device_id_type=MESH)

    pair_in = pair_copy(in_ref, w_in.at[chan], 0)
    pair_pix = pair_copy(pix_ref, pix.at[chan], 1)
    pair_up = pair_copy(up_ref, w_up.at[chan], 2)
    load_lat.wait()
    blocks = tokens.shape[0]
    whole = shard_len // LANES
    rest = shard_len - whole * LANES
    for b in list(range(MARGIN)) + list(range(MARGIN + whole, blocks)):
        tokens[b] = jnp.zeros((C_LAT, LANES), jnp.float32)
    for b in range(whole):
        tokens[MARGIN + b] = lat[:, b * LANES:(b + 1) * LANES].astype(jnp.float32)
    if rest:
        tokens[MARGIN + whole, :, 0:rest] = lat[:, whole * LANES:].astype(jnp.float32)

    part_start = seq % per_frame * shard_len
    limit = (blocks - 2) * LANES + LANES - 1

    load_anchor.wait()
    received[seq_size + seq] = pick_windows(tokens, anchors_cur, seq, slots, part_start, limit)
    pair_in.start()
    pair_pix.start()
    pair_up.start()

    def serve_next(to):
        anchor_back((seq - to + seq_size) % seq_size).wait_recv()
        send_next[to] = pick_windows(tokens, anchors_next, to, slots, part_start, limit)
        window_on((to - seq + seq_size) % seq_size).start()

    @pl.loop(0, seq_size - 1)
    def _(i):
        to = near_to_far(i)
        anchor_copy((seq - to + seq_size) % seq_size).wait_recv()
        send_cur[to] = pick_windows(tokens, anchors_cur, to, slots, part_start, limit)
        window_copy((to - seq + seq_size) % seq_size).start()

    @pl.when(has_next)
    def _():
        serve_next(seq)

        @pl.loop(0, seq_size - 1)
        def _(i):
            serve_next(near_to_far(i))

    load_pix.wait()
    pair_pix.wait_recv()
    cells = HELD * TH * TW
    spread[...] = jnp.zeros(spread.shape, jnp.bfloat16)
    row = lax.broadcasted_iota(jnp.int32, (TH * TW, LANES), 0)
    col = lax.broadcasted_iota(jnp.int32, (TH * TW, LANES), 1)
    for i in range(4):
        target = (2 * (row >> 4) + i // 2) * (2 * TW) + 2 * (row & 15) + i % 2
        chosen = (target == col).astype(jnp.float32).astype(jnp.bfloat16)
        for j in range(HELD):
            at = i * cells + j * TH * TW
            spread[at:at + TH * TW, j * LANES:(j + 1) * LANES] = chosen
    k_id = lax.broadcasted_iota(jnp.int32, (32, 12), 1)
    o_id = lax.broadcasted_iota(jnp.int32, (32, 12), 0)
    order = ((k_id >> 2) + (k_id & 3) * 8 == o_id).astype(jnp.float32).astype(jnp.bfloat16)
    to_pix = jnp.dot(
        order, jnp.concatenate([pix[0], pix[1]], axis=1), preferred_element_type=jnp.float32).astype(jnp.bfloat16)

    load_in.wait()
    pair_in.wait_recv()
    load_up.wait()
    pair_up.wait_recv()
    for step in range(1, seq_size):
        window_copy(step).wait_recv()

    @pl.when(has_prev)
    def _():
        for step in range(seq_size):
            window_on(step).wait_recv()

    lane = lax.broadcasted_iota(jnp.int32, (C_LAT, LANES), 1)
    win_row, win_col = grid_of(lane)
    hid_ids = lax.broadcasted_iota(jnp.int32, (HID_ROWS, LANES), 0)
    hid_row, hid_col = grid_of(hid_ids)
    halves = []
    for j in range(HELD):
        f0, y0, x0 = (anchors_cur[seq, i, 0, slots + j] for i in range(3))
        row_at, col_at = hid_row + (y0 - 1), hid_col + (x0 - 1)
        keep = (row_at >= 0) & (row_at < H_LAT) & (col_at >= 0) & (col_at < W_LAT)
        halves.append(jnp.where(keep, 0.5, 0.0))
        row_at, col_at = win_row + (y0 - 2), win_col + (x0 - 2)
        keep = (row_at >= 0) & (row_at < H_LAT) & (col_at >= 0) & (col_at < W_LAT) & (win_row < WIN_H)
        token = row_at * W_LAT + col_at
        for k in range(WIN_F):
            window = jnp.zeros((C_LAT, LANES), jnp.float32)
            for part in range(per_frame):
                held = received[(f0 + k) * per_frame + part, pl.ds(j * C_LAT, C_LAT), :].astype(jnp.float32)
                mine = keep
                if per_frame > 1:
                    mine = keep & (token >= part * shard_len) & (token < (part + 1) * shard_len)
                window = jnp.where(mine, held, window)
            for b in range(3):
                for c in range(3):
                    shift = b * WIN_W + c
                    moved = window if shift == 0 else pltpu.roll(window, LANES - shift, 1)
                    moved = moved.astype(jnp.bfloat16)
                    for a in range(3):
                        t = k - a
                        if 0 <= t < HID_F:
                            tap = (a * 3 + b) * 3 + c
                            patches[j * HID_F + t, pl.ds(tap * C_LAT, C_LAT), :] = moved

    for i in range(HELD * HID_F):
        rows_in[i * HID_ROWS:(i + 1) * HID_ROWS, :] = patches[i].T[:HID_ROWS]
    for half in range(2):
        pre = jnp.dot(rows_in[...], w_in[half], preferred_element_type=jnp.float32)
        for i in range(HELD * HID_F):
            for part in range(2):
                piece = pre[i * HID_ROWS:(i + 1) * HID_ROWS, part * LANES:(part + 1) * LANES]
                hidden[i, half * 2 + part, :, :] = gate(piece * halves[i // HID_F])

    rows = []
    for j in range(HELD):
        for y in range(TH):
            pieces = [
                hidden[j * HID_F + a, part, (y + b) * WIN_W + c:(y + b) * WIN_W + c + TW, :]
                for a in range(3) for b in range(3) for c in range(3) for part in range(C_MID // LANES)
            ]
            rows.append(jnp.concatenate(pieces, axis=1).astype(jnp.bfloat16))
    rows = jnp.concatenate(rows, axis=0)
    cut = TAPS * C_MID // 2
    total = sum(
        0.5 * jnp.dot(
            rows[:, lo:hi], jnp.concatenate([w_up[0, lo:hi, :], w_up[1, lo:hi, :]], axis=1),
            preferred_element_type=jnp.float32)
        for lo, hi in ((0, cut), (cut, TAPS * C_MID)))
    upper = gate(total).astype(jnp.bfloat16)
    colors = lax.dot_general(
        to_pix, upper, (((1,), (1,)), ((), ())), preferred_element_type=jnp.float32)
    wide = jnp.concatenate([colors[8 * i:8 * (i + 1)] for i in range(4)], axis=1).astype(jnp.bfloat16)
    parts[chan] = jnp.dot(wide, spread[...], preferred_element_type=jnp.float32)
    pair_out = pair_copy(parts.at[chan], parts.at[chan], 3)
    pair_out.start()

    pair_in.wait_send()
    pair_pix.wait_send()
    pair_up.wait_send()
    for step in range(1, seq_size):
        anchor_copy(step).wait_send()
        window_copy(step).wait_send()

    @pl.when(has_prev)
    def _():
        for step in range(seq_size):
            anchor_back(step).wait_send()

    @pl.when(has_next)
    def _():
        for step in range(seq_size):
            window_on(step).wait_send()

    pair_out.wait()
    live = lax.broadcasted_iota(jnp.int32, (MAXT, LANES), 0) < count_ref[0, 0]
    for e in range(3):
        tiles = [parts[j // HELD, e:e + 1, j % HELD * LANES:(j % HELD + 1) * LANES] for j in range(MAXT)]
        out_ref[e] = jnp.where(live, jnp.concatenate(tiles, axis=0), 0.0).astype(jnp.bfloat16)


def local(latents, conv_in, conv_up, to_pixels, slot_anchor, slot_count):
    seq_size = lax.axis_size("seq")
    tm_size = lax.axis_size("tm")
    shard_len = latents.shape[2]
    blocks = MARGIN + (shard_len + LANES - 1) // LANES + 3
    dma = pltpu.SemaphoreType.DMA
    vmem = pl.BlockSpec(memory_space=pltpu.VMEM)
    hbm = pl.BlockSpec(memory_space=pltpu.HBM)
    result = pl.pallas_call(
        functools.partial(kernel, (seq_size, tm_size, shard_len)),
        out_shape=pltpu.VMEM((3, MAXT, LANES), jnp.bfloat16),
        in_specs=[hbm] * 5 + [pl.BlockSpec(memory_space=pltpu.SMEM)],
        out_specs=vmem,
        scratch_shapes=[
            pltpu.VMEM((C_LAT, shard_len), jnp.bfloat16),
            pltpu.VMEM((2,) + to_pixels.shape[::-1], jnp.bfloat16),
            pltpu.VMEM((blocks, C_LAT, LANES), jnp.float32),
            pltpu.SMEM((seq_size, 3, 1, MAXT), jnp.int32),
            pltpu.SMEM((seq_size, 3, 1, MAXT), jnp.int32),
            pltpu.VMEM((seq_size, HELD * C_LAT, LANES), jnp.bfloat16),
            pltpu.VMEM((seq_size, HELD * C_LAT, LANES), jnp.bfloat16),
            pltpu.VMEM((2 * seq_size, HELD * C_LAT, LANES), jnp.bfloat16),
            pltpu.VMEM((2, TAPS * C_LAT, 256), jnp.bfloat16),
            pltpu.VMEM((2, TAPS * C_MID, LANES), jnp.bfloat16),
            pltpu.VMEM((HELD * HID_F, TAPS * C_LAT, LANES), jnp.bfloat16),
            pltpu.VMEM((HELD * HID_F * HID_ROWS, TAPS * C_LAT), jnp.bfloat16),
            pltpu.VMEM((HELD * HID_F, C_MID // LANES, HID_ROWS, LANES), jnp.float32),
            pltpu.VMEM((4 * HELD * TH * TW, HELD * LANES), jnp.bfloat16),
            pltpu.VMEM((2, 8, HELD * LANES), jnp.float32),
            dma((seq_size,)), dma((seq_size,)), dma((seq_size,)), dma((seq_size,)),
            dma((seq_size,)), dma((seq_size,)), dma((seq_size,)), dma((seq_size,)),
            dma((6,)), dma((8,)),
        ],
        compiler_params=pltpu.CompilerParams(collective_id=0, has_side_effects=True),
        name="decode",
    )(
        latents[0], conv_in.reshape(TAPS * C_LAT, -1), conv_up.reshape(TAPS * C_MID, -1),
        to_pixels.T, slot_anchor.transpose(1, 0, 2), slot_count)
    return result.transpose(1, 0, 2)[None, :, :, None, :]


def solution(mesh):
    placed = (
        P(("clip", "tm"), None, "seq"),
        P(None, None, None, None, "chan"),
        P(None, None, None, None, "chan"),
        P("chan", None),
        P(("clip", "tm"), None, "seq"),
        P(("clip", "tm"), "seq"),
    )
    return jax.shard_map(
        local,
        mesh=mesh,
        in_specs=placed,
        out_specs=P(("clip", "tm"), "seq", None, None, None),
        check_vma=False,
    )
```
